32 devices in a mesh: pix: 4 (over x, core), scan: 8 (over z, y).
Axes of the slice: x: 2, y: 2, z: 4, core: 2. Of those that a mesh axis runs over, the one named last changes fastest.
Arguments:
- scan_data: bfloat16 [128, 512, 512], P('pix', 'scan'), may hold values from -6 to 6
- pixel_coords: int32 [2, 128], P(None, 'pix'), may hold values from -6 to 6, as said below
- aberrations: float32 [4], replicated, may hold values from -3 to 3
Outputs:
- object_wave: float32 [2, 512, 512], P(None, 'scan', 'pix')
The draws below stay inside these ranges and needn't reach their ends.
Inputs may be any that keep to these rules, and one draw needn't show every extreme that they name: `pixel_coords`: each column is a distinct pair (u, v) of integers with u * u + v * v <= 40; their order is arbitrary.
All inputs are finite; a program needn't handle non-finite values.
Results may differ from the reference program's by a relative error of at most 0.0043.
Values may be sent and summed in bfloat16 or wider, within the bound.
A program may use at most 64 MiB of HBM per device.

```python
import math
import jax
import jax.numpy as jnp
from jax import lax

NX = 512
NY = 512
PIXELS = 128
STEP = 8


def draw_pixel_coords(key, part):
    lattice = jnp.arange(169, dtype=jnp.int32)
    along_u = lattice // 13 - 6
    along_v = lattice % 13 - 6
    inside = (along_u * along_u + along_v * along_v <= 40).astype(jnp.int32)
    shuffled = jax.random.permutation(key, 169).astype(jnp.int32)
    scores = inside * 1000 + shuffled
    ranking = jnp.argsort(-scores, stable=True)[:PIXELS]
    return jnp.stack([along_u[ranking], along_v[ranking]]).astype(jnp.int32)


def shard_levels(own_key, shape, shards, least, largest):
    loudness = 1.0
    for dim, parts in shards:
        heights = jax.random.uniform(jax.random.fold_in(jax.random.fold_in(own_key, 6), dim), (parts,), jnp.float32, least / len(shards), largest / len(shards))
        loudness = loudness * jnp.repeat(jnp.exp(heights), shape[dim] // parts).reshape((-1,) + (1,) * (len(shape) - 1 - dim))
    return loudness


def scatter_about(key, shape, width, most, cuts=(), held_as=jnp.bfloat16):
    result = width * jax.random.normal(key, shape, jnp.float32)
    if cuts:
        result = result * shard_levels(key, shape, cuts, -0.22, 0.18)
    return jnp.clip(result, -most, most).astype(held_as)


def setup_inputs(seed: int = 0) -> dict:
    keys = jax.random.split(jax.random.key(seed), 4)
    return {
        "scan_data": scatter_about(keys[0], (PIXELS, NX, NY), 1.0, 6.0, ((0, 4), (1, 8))),
        "pixel_coords": draw_pixel_coords(jax.random.fold_in(keys[3], 71), 0),
        "aberrations": jnp.clip(jax.random.uniform(keys[2], (4,), jnp.float32, -3.0, 3.0), -3.0, 3.0),
    }


full_turn = 2.0 * math.pi


def frequencies(length, banded):
    counter = jnp.arange(length // 2 if banded else length, dtype=jnp.int32)
    if banded:
        return jnp.where(counter < length // 4, counter, counter + length // 2).astype(jnp.int32)
    return counter


def signed_freq(spectral, length):
    return jnp.where(spectral < length // 2, spectral, spectral - length).astype(jnp.int32)


def phase_table(spectral, length, places):
    product = (spectral[:, None] * places[None, :]) % length
    angles = product.astype(jnp.float32) * (full_turn / length)
    return jnp.cos(angles), jnp.sin(angles)


def aberration(along_x, along_y, coefficients):
    aperture = 40.0 * STEP * STEP
    radial = (along_x * along_x + along_y * along_y) / aperture
    return (coefficients[0] * radial
            + coefficients[1] * (along_x * along_x - along_y * along_y) / aperture
            + coefficients[2] * 2.0 * along_x * along_y / aperture
            + coefficients[3] * radial * radial)


def trotter(column_u, column_v, freq_x, freq_y, coefficients):
    centre_x = STEP * column_u
    centre_y = STEP * column_v
    minus_x = centre_x - freq_x
    minus_y = centre_y - freq_y
    plus_x = centre_x + freq_x
    plus_y = centre_y + freq_y
    aperture_bound = 40 * STEP * STEP
    inside_minus = minus_x * minus_x + minus_y * minus_y <= aperture_bound
    inside_plus = plus_x * plus_x + plus_y * plus_y <= aperture_bound
    left_mask = jnp.logical_and(inside_minus, jnp.logical_not(inside_plus)).astype(jnp.float32)
    right_mask = jnp.logical_and(inside_plus, jnp.logical_not(inside_minus)).astype(jnp.float32)
    own_phase = aberration(centre_x.astype(jnp.float32), centre_y.astype(jnp.float32), coefficients)
    left_phase = aberration(minus_x.astype(jnp.float32), minus_y.astype(jnp.float32), coefficients) - own_phase
    right_phase = own_phase - aberration(plus_x.astype(jnp.float32), plus_y.astype(jnp.float32), coefficients)
    weight_real = left_mask * jnp.cos(left_phase) - right_mask * jnp.cos(right_phase)
    weight_imag = left_mask * jnp.sin(left_phase) - right_mask * jnp.sin(right_phase)
    return weight_real, weight_imag


def rounded(table):
    return lax.optimization_barrier(table.astype(jnp.bfloat16)).astype(jnp.float32)


def reference(scan_data, pixel_coords, aberrations):
    highest = lax.Precision.HIGHEST
    across = frequencies(NY, True)
    downward = frequencies(NX, True)
    cosine_rows, sine_rows = phase_table(jnp.arange(NY, dtype=jnp.int32), NY, across)
    cosine_rows = rounded(cosine_rows)
    sine_rows = rounded(sine_rows)
    inverse_cos_x, inverse_sin_x = phase_table(downward, NX, jnp.arange(NX, dtype=jnp.int32))
    cosine_cols = rounded(inverse_cos_x)
    sine_cols = rounded(inverse_sin_x)
    freq_x = signed_freq(downward, NX)[:, None]
    freq_y = signed_freq(across, NY)[None, :]

    def accumulate(totals, inputs):
        picture, coords = inputs
        picture = picture.astype(jnp.float32)
        real_rows = jnp.dot(picture, cosine_rows, precision=highest, preferred_element_type=jnp.float32).astype(jnp.bfloat16)
        imag_rows = (-jnp.dot(picture, sine_rows, precision=highest, preferred_element_type=jnp.float32)).astype(jnp.bfloat16)
        real_rows, imag_rows = lax.optimization_barrier((real_rows, imag_rows))
        real_rows = real_rows.astype(jnp.float32)
        imag_rows = imag_rows.astype(jnp.float32)
        spec_real = (jnp.dot(cosine_cols, real_rows, precision=highest, preferred_element_type=jnp.float32)
                     + jnp.dot(sine_cols, imag_rows, precision=highest, preferred_element_type=jnp.float32))
        spec_imag = (jnp.dot(cosine_cols, imag_rows, precision=highest, preferred_element_type=jnp.float32)
                     - jnp.dot(sine_cols, real_rows, precision=highest, preferred_element_type=jnp.float32))
        weight_real, weight_imag = trotter(coords[0], coords[1], freq_x, freq_y, aberrations)
        return (totals[0] + spec_real * weight_real - spec_imag * weight_imag,
                totals[1] + spec_real * weight_imag + spec_imag * weight_real), None

    initial = jnp.zeros((downward.shape[0], across.shape[0]), jnp.float32)
    (summed_real, summed_imag), _ = lax.scan(accumulate, (initial, initial), (scan_data, pixel_coords.T))
    column_real = (jnp.dot(inverse_cos_x.T, summed_real, precision=highest, preferred_element_type=jnp.float32)
                   - jnp.dot(inverse_sin_x.T, summed_imag, precision=highest, preferred_element_type=jnp.float32))
    column_imag = (jnp.dot(inverse_sin_x.T, summed_real, precision=highest, preferred_element_type=jnp.float32)
                   + jnp.dot(inverse_cos_x.T, summed_imag, precision=highest, preferred_element_type=jnp.float32))
    final_cos, final_sin = phase_table(across, NY, jnp.arange(NY, dtype=jnp.int32))
    object_real = (jnp.dot(column_real, final_cos, precision=highest, preferred_element_type=jnp.float32)
                   - jnp.dot(column_imag, final_sin, precision=highest, preferred_element_type=jnp.float32))
    object_imag = (jnp.dot(column_real, final_sin, precision=highest, preferred_element_type=jnp.float32)
                   + jnp.dot(column_imag, final_cos, precision=highest, preferred_element_type=jnp.float32))
    return jnp.stack([object_real, object_imag]) * (1.0 / (NX * NY))
```

```python
import functools
import math

import jax
import jax.numpy as jnp
import numpy as np
from jax import lax
from jax.experimental import pallas as pl
from jax.experimental.pallas import tpu as pltpu
from jax.sharding import PartitionSpec as P

STEP = 8
EXTENT = 6
REACH = STEP * EXTENT
APERTURE = 40 * STEP * STEP


def centred(length):
    return np.arange(length // 2) - length // 4


def table_pair(freqs, places, length):
    angles = (np.outer(freqs, places) % length) * (2.0 * math.pi / length)
    return np.cos(angles), np.sin(angles)


def aberration(px, py, a):
    px = px.astype(jnp.float32)
    py = py.astype(jnp.float32)
    radial = (px * px + py * py) / float(APERTURE)
    return (
        a[0] * radial
        + a[1] * (px * px - py * py) / float(APERTURE)
        + a[2] * 2.0 * px * py / float(APERTURE)
        + a[3] * radial * radial
    )


def partial_kernel(
    group, rows, coords, aber, data, forward, columns, out, base_re, base_im, tab_re, tab_im, spec
):
    step = pl.program_id(0)
    band_x = out.shape[1]
    band_y = out.shape[2]
    shifts = tab_re.shape[0]
    coeffs = [aber[i] for i in range(4)]

    @pl.when(step == 0)
    def _():
        out[...] = jnp.zeros_like(out)
        tall, wide = base_re.shape
        chunk = 16

        @pl.loop(0, tall // chunk)
        def _(i):
            at = pl.ds(pl.multiple_of(i * chunk, chunk), chunk)
            px = lax.broadcasted_iota(jnp.int32, (chunk, wide), 0) + (
                i * chunk - band_x // 2 - REACH
            )
            py = lax.broadcasted_iota(jnp.int32, (chunk, wide), 1) - (band_y // 2 + REACH)
            inside = px * px + py * py <= APERTURE
            phase = aberration(px, py, coeffs)
            real = jnp.cos(phase)
            real = jnp.where(real == 0.0, 1e-12, real)
            base_re[at, :] = jnp.where(inside, real, 0.0)
            base_im[at, :] = jnp.where(inside, jnp.sin(phase), 0.0)
            for s in range(shifts):
                tab_re[s, at, :] = base_re[at, STEP * s : STEP * s + band_y]
                tab_im[s, at, :] = base_im[at, STEP * s : STEP * s + band_y]

    me = lax.axis_index("scan")
    table = columns[me]
    rowspec = jnp.dot(data[...], forward[...], preferred_element_type=jnp.float32)

    def transform(g):
        mine = rowspec[g * rows : (g + 1) * rows].astype(jnp.bfloat16)
        turned = jnp.concatenate([mine[:, band_y:], -mine[:, :band_y]], axis=1)
        if rows % 16 == 0:
            both = jnp.concatenate([mine, turned], axis=0)
            spec[g] = jnp.dot(table, both, preferred_element_type=jnp.float32)
        else:
            spec[g] = jnp.dot(
                table[:, :rows], mine, preferred_element_type=jnp.float32
            ) + jnp.dot(table[:, rows:], turned, preferred_element_type=jnp.float32)

    def weigh(g):
        pixel = step * group + g
        u = coords[0, pixel]
        v = coords[1, pixel]
        kx = jnp.full((8, 128), STEP * u, jnp.int32)
        ky = jnp.full((8, 128), STEP * v, jnp.int32)
        own = aberration(kx, ky, coeffs)
        cos_own = jnp.concatenate([jnp.cos(own)] * (band_y // 128), axis=1)
        sin_own = jnp.concatenate([jnp.sin(own)] * (band_y // 128), axis=1)
        for r in range(0, band_x, 8):
            left = pl.ds(pl.multiple_of(r + REACH - STEP * u, 8), 8)
            right = pl.ds(pl.multiple_of(r + REACH + STEP * u, 8), 8)
            ar = tab_re[EXTENT - v, left, :]
            ai = tab_im[EXTENT - v, left, :]
            br = tab_re[EXTENT + v, right, :]
            bi = tab_im[EXTENT + v, right, :]
            both = ar * br != 0.0
            wr = cos_own * (ar - br) + sin_own * (ai - bi)
            wi = cos_own * (ai + bi) - sin_own * (ar + br)
            wr = jnp.where(both, 0.0, wr)
            wi = jnp.where(both, 0.0, wi)
            sr = spec[g, r : r + 8, :band_y]
            si = spec[g, r : r + 8, band_y:]
            out[0, r : r + 8, :] += sr * wr - si * wi
            out[1, r : r + 8, :] += sr * wi + si * wr

    transform(0)
    for g in range(group):
        if g + 1 < group:
            transform(g + 1)
        weigh(g)


def partial_spectrum(scan_data, pixel_coords, aberrations, scan_count):
    pixels, rows, breadth = scan_data.shape
    height = rows * scan_count
    band_x, band_y = height // 2, breadth // 2
    group = 4
    fc, fs = table_pair(centred(breadth), np.arange(breadth), breadth)
    forward = jnp.asarray(np.concatenate([fc.T, -fs.T], axis=1), jnp.bfloat16)
    cc, cs = table_pair(centred(height), np.arange(height), height)
    stacked = np.stack(
        [
            np.concatenate([cc[:, i : i + rows], cs[:, i : i + rows]], axis=1)
            for i in range(0, height, rows)
        ]
    )
    columns = jnp.asarray(stacked, jnp.bfloat16)
    tall = band_x + 2 * REACH
    wide = -(-(band_y + 2 * REACH) // 128) * 128
    whole = lambda shape: pl.BlockSpec(shape, lambda i: (0,) * len(shape))
    shifts = 2 * EXTENT + 1
    return pl.pallas_call(
        functools.partial(partial_kernel, group, rows),
        grid=(pixels // group,),
        out_shape=jax.ShapeDtypeStruct((2, band_x, band_y), jnp.float32),
        in_specs=[
            pl.BlockSpec(memory_space=pltpu.SMEM),
            pl.BlockSpec(memory_space=pltpu.SMEM),
            pl.BlockSpec((group * rows, breadth), lambda i: (i, 0)),
            whole(forward.shape),
            whole(columns.shape),
        ],
        out_specs=whole((2, band_x, band_y)),
        scratch_shapes=[
            pltpu.VMEM((tall, wide), jnp.float32),
            pltpu.VMEM((tall, wide), jnp.float32),
            pltpu.VMEM((shifts, tall, band_y), jnp.float32),
            pltpu.VMEM((shifts, tall, band_y), jnp.float32),
            pltpu.VMEM((group, band_x, 2 * band_y), jnp.float32),
        ],
        compiler_params=pltpu.CompilerParams(vmem_limit_bytes=60 * 1024 * 1024),
        name="partial_spectrum",
    )(pixel_coords, aberrations, scan_data.reshape(pixels * rows, breadth), forward, columns)


def on_device(scan_data, pixel_coords, aberrations):
    highest = lax.Precision.HIGHEST
    pixels, rows, breadth = scan_data.shape
    scan_count = lax.axis_size("scan")
    pix_count = lax.axis_size("pix")
    height = rows * scan_count
    partial = partial_spectrum(scan_data, pixel_coords, aberrations, scan_count)
    total = lax.psum(partial, ("pix", "scan"))
    share = breadth // pix_count
    ic, isn = table_pair(centred(height), np.arange(height), height)
    inverse_x = jnp.asarray(np.stack([ic, isn]), jnp.float32)
    inverse_x = lax.dynamic_slice_in_dim(inverse_x, lax.axis_index("scan") * rows, rows, 2)
    jc, js = table_pair(centred(breadth), np.arange(breadth), breadth)
    inverse_y = jnp.asarray(np.stack([jc, js]), jnp.float32)
    inverse_y = lax.dynamic_slice_in_dim(inverse_y, lax.axis_index("pix") * share, share, 2)
    dot = functools.partial(jnp.einsum, precision=highest)
    left = dot("tkx,pkq->tpxq", inverse_x, total)
    mid_re = left[0, 0] - left[1, 1]
    mid_im = left[1, 0] + left[0, 1]
    mid = jnp.stack([mid_re, mid_im])
    right = dot("pxq,tqy->tpxy", mid, inverse_y)
    result = jnp.stack([right[0, 0] - right[1, 1], right[1, 0] + right[0, 1]])
    return result * (1.0 / (height * breadth))


def solution(mesh):
    placed = (P("pix", "scan", None), P(None, "pix"), P())
    return jax.shard_map(
        on_device, mesh=mesh, in_specs=placed, out_specs=P(None, "scan", "pix"), check_vma=False
    )
```

```python
import functools
import math

import jax
import jax.numpy as jnp
import numpy as np
from jax import lax
from jax.experimental import pallas as pl
from jax.experimental.pallas import tpu as pltpu
from jax.sharding import PartitionSpec as P

STEP = 8
EXTENT = 6
REACH = STEP * EXTENT
APERTURE = 40 * STEP * STEP


def centred(length):
    return np.arange(length // 2) - length // 4


def table_pair(freqs, places, length):
    angles = (np.outer(freqs, places) % length) * (2.0 * math.pi / length)
    return np.cos(angles), np.sin(angles)


def aberration(px, py, a):
    px = px.astype(jnp.float32)
    py = py.astype(jnp.float32)
    radial = (px * px + py * py) / float(APERTURE)
    return (
        a[0] * radial
        + a[1] * (px * px - py * py) / float(APERTURE)
        + a[2] * 2.0 * px * py / float(APERTURE)
        + a[3] * radial * radial
    )


def partial_kernel(
    group, rows, coords, aber, data, forward, columns, final, base_re, base_im, tab_re, tab_im, spec, out
):
    step = pl.program_id(0)
    band_x, band_y = out.shape[1:]
    shifts = tab_re.shape[0]
    coeffs = [aber[i] for i in range(4)]

    @pl.when(step == 0)
    def _():
        out[...] = jnp.zeros_like(out)
        tall, wide = base_re.shape
        chunk = 16

        @pl.loop(0, tall // chunk)
        def _(i):
            at = pl.ds(pl.multiple_of(i * chunk, chunk), chunk)
            px = lax.broadcasted_iota(jnp.int32, (chunk, wide), 0) + (
                i * chunk - band_x // 2 - REACH
            )
            py = lax.broadcasted_iota(jnp.int32, (chunk, wide), 1) - (band_y // 2 + REACH)
            inside = px * px + py * py <= APERTURE
            phase = aberration(px, py, coeffs)
            real = jnp.cos(phase)
            real = jnp.where(real == 0.0, 1e-12, real)
            base_re[at, :] = jnp.where(inside, real, 0.0)
            base_im[at, :] = jnp.where(inside, jnp.sin(phase), 0.0)
            for s in range(shifts):
                tab_re[s, at, :] = base_re[at, STEP * s : STEP * s + band_y]
                tab_im[s, at, :] = base_im[at, STEP * s : STEP * s + band_y]

    me = lax.axis_index("scan")
    table = columns[me]
    rowspec = jnp.dot(data[...], forward[...], preferred_element_type=jnp.float32)

    def transform(g):
        mine = rowspec[g * rows : (g + 1) * rows].astype(jnp.bfloat16)
        turned = jnp.concatenate([mine[:, band_y:], -mine[:, :band_y]], axis=1)
        if rows % 16 == 0:
            both = jnp.concatenate([mine, turned], axis=0)
            spec[g] = jnp.dot(table, both, preferred_element_type=jnp.float32)
        else:
            spec[g] = jnp.dot(
                table[:, :rows], mine, preferred_element_type=jnp.float32
            ) + jnp.dot(table[:, rows:], turned, preferred_element_type=jnp.float32)

    def weigh(g):
        pixel = step * group + g
        u = coords[0, pixel]
        v = coords[1, pixel]
        kx = jnp.full((8, 128), STEP * u, jnp.int32)
        ky = jnp.full((8, 128), STEP * v, jnp.int32)
        own = aberration(kx, ky, coeffs)
        cos_own = jnp.concatenate([jnp.cos(own)] * (band_y // 128), axis=1)
        sin_own = jnp.concatenate([jnp.sin(own)] * (band_y // 128), axis=1)
        for r in range(0, band_x, 8):
            left = pl.ds(pl.multiple_of(r + REACH - STEP * u, 8), 8)
            right = pl.ds(pl.multiple_of(r + REACH + STEP * u, 8), 8)
            ar = tab_re[EXTENT - v, left, :]
            ai = tab_im[EXTENT - v, left, :]
            br = tab_re[EXTENT + v, right, :]
            bi = tab_im[EXTENT + v, right, :]
            both = ar * br != 0.0
            wr = cos_own * (ar - br) + sin_own * (ai - bi)
            wi = cos_own * (ai + bi) - sin_own * (ar + br)
            wr = jnp.where(both, 0.0, wr)
            wi = jnp.where(both, 0.0, wi)
            sr = spec[g, r : r + 8, :band_y]
            si = spec[g, r : r + 8, band_y:]
            out[0, r : r + 8, :] += sr * wr - si * wi
            out[1, r : r + 8, :] += sr * wi + si * wr

    transform(0)
    for g in range(group):
        if g + 1 < group:
            transform(g + 1)
        weigh(g)

    @pl.when(step == pl.num_programs(0) - 1)
    def _():
        final[...] = out[...].astype(final.dtype)


def sum_kernel(count, width, part, total, arrived, own, send_a, take_a, send_b, take_b):
    me = lax.axis_index("pix") * width + lax.axis_index("scan")

    def place(k):
        other = lax.rem(me + k, count)
        return other, {"pix": other // width, "scan": lax.rem(other, width)}

    barrier = pltpu.get_barrier_semaphore()

    @pl.loop(1, count)
    def _(k):
        pl.semaphore_signal(
            barrier, inc=1, device_id=place(k)[1], device_id_type=pl.DeviceIdType.MESH
        )

    pl.semaphore_wait(barrier, count - 1)

    def scatter(k):
        other, where = place(k)
        return pltpu.make_async_remote_copy(
            src_ref=part.at[other],
            dst_ref=arrived.at[k],
            send_sem=send_a.at[k],
            recv_sem=take_a.at[k],
            device_id=where,
            device_id_type=pl.DeviceIdType.MESH,
        )

    def gather(k):
        return pltpu.make_async_remote_copy(
            src_ref=own,
            dst_ref=total.at[me],
            send_sem=send_b.at[k],
            recv_sem=take_b.at[k],
            device_id=place(k)[1],
            device_id_type=pl.DeviceIdType.MESH,
        )

    @pl.loop(1, count)
    def _(k):
        scatter(k).start()

    def add(k, summed):
        scatter(k).wait_recv()
        return summed + arrived[k].astype(jnp.float32)

    summed = lax.fori_loop(1, count, add, part[me].astype(jnp.float32))
    own[...] = summed.astype(own.dtype)
    total[me] = own[...]

    @pl.loop(1, count)
    def _(k):
        gather(k).start()

    @pl.loop(1, count)
    def _(k):
        scatter(k).wait_send()
        gather(k).wait()


def sum_everywhere(partial):
    width = lax.axis_size("scan")
    count = lax.axis_size("pix") * width
    parts, band_x, band_y = partial.shape
    lines = parts * band_x // count
    if parts * band_x % (16 * count):
        return lax.psum(partial.astype(jnp.float32), ("pix", "scan"))
    pieces = (count, lines, band_y)
    vmem = pl.BlockSpec(memory_space=pltpu.VMEM)
    total = pl.pallas_call(
        functools.partial(sum_kernel, count, width),
        out_shape=jax.ShapeDtypeStruct(pieces, partial.dtype),
        in_specs=[vmem],
        out_specs=vmem,
        scratch_shapes=[
            pltpu.VMEM(pieces, partial.dtype),
            pltpu.VMEM(pieces[1:], partial.dtype),
        ]
        + [pltpu.SemaphoreType.DMA((count,))] * 4,
        compiler_params=pltpu.CompilerParams(collective_id=0, has_side_effects=True),
        name="sum_everywhere",
    )(partial.reshape(pieces))
    return total.reshape(partial.shape).astype(jnp.float32)


def partial_spectrum(scan_data, pixel_coords, aberrations, scan_count):
    pixels, rows, breadth = scan_data.shape
    height = rows * scan_count
    band_x, band_y = height // 2, breadth // 2
    group = 4
    fc, fs = table_pair(centred(breadth), np.arange(breadth), breadth)
    forward = jnp.asarray(np.concatenate([fc.T, -fs.T], axis=1), jnp.bfloat16)
    cc, cs = table_pair(centred(height), np.arange(height), height)
    stacked = np.stack(
        [
            np.concatenate([cc[:, i : i + rows], cs[:, i : i + rows]], axis=1)
            for i in range(0, height, rows)
        ]
    )
    columns = jnp.asarray(stacked, jnp.bfloat16)
    tall = band_x + 2 * REACH
    wide = -(-(band_y + 2 * REACH) // 128) * 128
    whole = lambda shape: pl.BlockSpec(shape, lambda i: (0,) * len(shape))
    shifts = 2 * EXTENT + 1
    return pl.pallas_call(
        functools.partial(partial_kernel, group, rows),
        grid=(pixels // group,),
        out_shape=jax.ShapeDtypeStruct((2, band_x, band_y), jnp.bfloat16),
        in_specs=[
            pl.BlockSpec(memory_space=pltpu.SMEM),
            pl.BlockSpec(memory_space=pltpu.SMEM),
            pl.BlockSpec((group * rows, breadth), lambda i: (i, 0)),
            whole(forward.shape),
            whole(columns.shape),
        ],
        out_specs=whole((2, band_x, band_y)),
        scratch_shapes=[
            pltpu.VMEM((tall, wide), jnp.float32),
            pltpu.VMEM((tall, wide), jnp.float32),
            pltpu.VMEM((shifts, tall, band_y), jnp.float32),
            pltpu.VMEM((shifts, tall, band_y), jnp.float32),
            pltpu.VMEM((group, band_x, 2 * band_y), jnp.float32),
            pltpu.VMEM((2, band_x, band_y), jnp.float32),
        ],
        compiler_params=pltpu.CompilerParams(vmem_limit_bytes=60 * 1024 * 1024),
        name="partial_spectrum",
    )(pixel_coords, aberrations, scan_data.reshape(pixels * rows, breadth), forward, columns)


def on_device(scan_data, pixel_coords, aberrations):
    highest = lax.Precision.HIGHEST
    pixels, rows, breadth = scan_data.shape
    scan_count = lax.axis_size("scan")
    pix_count = lax.axis_size("pix")
    height = rows * scan_count
    partial = partial_spectrum(scan_data, pixel_coords, aberrations, scan_count)
    total = sum_everywhere(partial)
    share = breadth // pix_count
    ic, isn = table_pair(centred(height), np.arange(height), height)
    inverse_x = jnp.asarray(np.stack([ic, isn]), jnp.float32)
    inverse_x = lax.dynamic_slice_in_dim(inverse_x, lax.axis_index("scan") * rows, rows, 2)
    jc, js = table_pair(centred(breadth), np.arange(breadth), breadth)
    inverse_y = jnp.asarray(np.stack([jc, js]), jnp.float32)
    inverse_y = lax.dynamic_slice_in_dim(inverse_y, lax.axis_index("pix") * share, share, 2)
    dot = functools.partial(jnp.einsum, precision=highest)
    left = dot("tkx,pkq->tpxq", inverse_x, total)
    mid_re = left[0, 0] - left[1, 1]
    mid_im = left[1, 0] + left[0, 1]
    mid = jnp.stack([mid_re, mid_im])
    right = dot("pxq,tqy->tpxy", mid, inverse_y)
    result = jnp.stack([right[0, 0] - right[1, 1], right[1, 0] + right[0, 1]])
    return result * (1.0 / (height * breadth))


def solution(mesh):
    placed = (P("pix", "scan", None), P(None, "pix"), P())
    return jax.shard_map(
        on_device, mesh=mesh, in_specs=placed, out_specs=P(None, "scan", "pix"), check_vma=False
    )
```

```python
import functools
import math

import jax
import jax.numpy as jnp
import numpy as np
from jax import lax
from jax.experimental import pallas as pl
from jax.experimental.pallas import tpu as pltpu
from jax.sharding import PartitionSpec as P

STEP = 8
EXTENT = 6
REACH = STEP * EXTENT
APERTURE = 40 * STEP * STEP


def centred(length):
    return np.arange(length // 2) - length // 4


def table_pair(freqs, places, length):
    angles = (np.outer(freqs, places) % length) * (2.0 * math.pi / length)
    return np.cos(angles), np.sin(angles)


def aberration(px, py, a):
    px = px.astype(jnp.float32)
    py = py.astype(jnp.float32)
    radial = (px * px + py * py) / float(APERTURE)
    return (
        a[0] * radial
        + a[1] * (px * px - py * py) / float(APERTURE)
        + a[2] * 2.0 * px * py / float(APERTURE)
        + a[3] * radial * radial
    )


def partial_kernel(
    group, rows, coords, aber, data, forward, columns, final, base_re, base_im, tab_re, tab_im, spec, out
):
    step = pl.program_id(0)
    band_x, band_y = out.shape[1:]
    shifts = tab_re.shape[0]
    coeffs = [aber[i] for i in range(4)]

    @pl.when(step == 0)
    def _():
        out[...] = jnp.zeros_like(out)
        tall, wide = base_re.shape
        chunk = 16

        @pl.loop(0, tall // chunk)
        def _(i):
            at = pl.ds(pl.multiple_of(i * chunk, chunk), chunk)
            px = lax.broadcasted_iota(jnp.int32, (chunk, wide), 0) + (
                i * chunk - band_x // 2 - REACH
            )
            py = lax.broadcasted_iota(jnp.int32, (chunk, wide), 1) - (band_y // 2 + REACH)
            inside = px * px + py * py <= APERTURE
            phase = aberration(px, py, coeffs)
            real = jnp.cos(phase)
            real = jnp.where(real == 0.0, 1e-12, real)
            base_re[at, :] = jnp.where(inside, real, 0.0)
            base_im[at, :] = jnp.where(inside, jnp.sin(phase), 0.0)
            for s in range(shifts):
                tab_re[s, at, :] = base_re[at, STEP * s : STEP * s + band_y]
                tab_im[s, at, :] = base_im[at, STEP * s : STEP * s + band_y]

    me = lax.axis_index("scan")
    table = columns[me]
    rowspec = jnp.dot(data[...], forward[...], preferred_element_type=jnp.float32)

    def transform(g):
        mine = rowspec[g * rows : (g + 1) * rows].astype(jnp.bfloat16)
        turned = jnp.concatenate([mine[:, band_y:], -mine[:, :band_y]], axis=1)
        if rows % 16 == 0:
            both = jnp.concatenate([mine, turned], axis=0)
            spec[g] = jnp.dot(table, both, preferred_element_type=jnp.float32)
        else:
            spec[g] = jnp.dot(
                table[:, :rows], mine, preferred_element_type=jnp.float32
            ) + jnp.dot(table[:, rows:], turned, preferred_element_type=jnp.float32)

    def weigh(g):
        pixel = step * group + g
        u = coords[0, pixel]
        v = coords[1, pixel]
        kx = jnp.full((8, 128), STEP * u, jnp.int32)
        ky = jnp.full((8, 128), STEP * v, jnp.int32)
        own = aberration(kx, ky, coeffs)
        cos_own = jnp.concatenate([jnp.cos(own)] * (band_y // 128), axis=1)
        sin_own = jnp.concatenate([jnp.sin(own)] * (band_y // 128), axis=1)
        for r in range(0, band_x, 8):
            left = pl.ds(pl.multiple_of(r + REACH - STEP * u, 8), 8)
            right = pl.ds(pl.multiple_of(r + REACH + STEP * u, 8), 8)
            ar = tab_re[EXTENT - v, left, :]
            ai = tab_im[EXTENT - v, left, :]
            br = tab_re[EXTENT + v, right, :]
            bi = tab_im[EXTENT + v, right, :]
            both = ar * br != 0.0
            wr = cos_own * (ar - br) + sin_own * (ai - bi)
            wi = cos_own * (ai + bi) - sin_own * (ar + br)
            wr = jnp.where(both, 0.0, wr)
            wi = jnp.where(both, 0.0, wi)
            sr = spec[g, r : r + 8, :band_y]
            si = spec[g, r : r + 8, band_y:]
            out[0, r : r + 8, :] += sr * wr - si * wi
            out[1, r : r + 8, :] += sr * wi + si * wr

    transform(0)
    for g in range(group):
        if g + 1 < group:
            transform(g + 1)
        weigh(g)

    @pl.when(step == pl.num_programs(0) - 1)
    def _():
        final[...] = out[...].astype(final.dtype)


def sum_kernel(across, along, part, total, arrived, held, crossed, own, block, *sems):
    scan_me = lax.axis_index("scan")
    pix_me = lax.axis_index("pix")

    def peer(axis, k):
        if axis == "scan":
            return lax.rem(scan_me + k, along)
        return lax.rem(pix_me + k, across)

    def copy(axis, k, source, target, stage):
        return pltpu.make_async_remote_copy(
            src_ref=source,
            dst_ref=target,
            send_sem=sems[2 * stage].at[k],
            recv_sem=sems[2 * stage + 1].at[k],
            device_id={axis: peer(axis, k)},
            device_id_type=pl.DeviceIdType.MESH,
        )

    barrier = pltpu.get_barrier_semaphore()
    for axis, count in (("scan", along), ("pix", across)):
        for k in range(1, count):
            pl.semaphore_signal(
                barrier,
                inc=1,
                device_id={axis: peer(axis, k)},
                device_id_type=pl.DeviceIdType.MESH,
            )
    pl.semaphore_wait(barrier, along + across - 2)

    pending = [
        copy("scan", k, part.at[peer("scan", k)], arrived.at[k], 0) for k in range(1, along)
    ]
    for c in pending:
        c.start()
    for c in pending:
        c.wait_recv()
    lines = own.shape[0]
    for j in range(across):
        rows = pl.ds(j * lines, lines)
        summed = part[scan_me, rows, :].astype(jnp.float32)
        for k in range(1, along):
            summed += arrived[k, rows, :].astype(jnp.float32)
        held[j] = summed.astype(held.dtype)

    second = [
        copy("pix", k, held.at[peer("pix", k)], crossed.at[k], 1) for k in range(1, across)
    ]
    for c in second:
        c.start()
    for c in second:
        c.wait_recv()
    summed = held[pix_me].astype(jnp.float32)
    for k in range(1, across):
        summed += crossed[k].astype(jnp.float32)
    own[...] = summed.astype(own.dtype)
    block[pix_me] = own[...]

    third = [copy("pix", k, own, block.at[pix_me], 2) for k in range(1, across)]
    for c in third:
        c.start()
    for c in third:
        c.wait_recv()

    fourth = [copy("scan", k, block, total.at[scan_me], 3) for k in range(1, along)]
    for c in fourth:
        c.start()
    total[scan_me] = block[...]
    for c in fourth:
        c.wait_recv()
    for c in pending + second + third + fourth:
        c.wait_send()


def sum_everywhere(partial):
    along = lax.axis_size("scan")
    across = lax.axis_size("pix")
    parts, band_x, band_y = partial.shape
    lines = parts * band_x // (along * across)
    if parts * band_x % (16 * along * across):
        return lax.psum(partial.astype(jnp.float32), ("pix", "scan"))
    narrow = jnp.bfloat16
    pieces = (along, across * lines, band_y)
    vmem = pl.BlockSpec(memory_space=pltpu.VMEM)
    total = pl.pallas_call(
        functools.partial(sum_kernel, across, along),
        out_shape=jax.ShapeDtypeStruct((along, across, lines, band_y), narrow),
        in_specs=[vmem],
        out_specs=vmem,
        scratch_shapes=[
            pltpu.VMEM(pieces, partial.dtype),
            pltpu.VMEM((across, lines, band_y), narrow),
            pltpu.VMEM((across, lines, band_y), narrow),
            pltpu.VMEM((lines, band_y), narrow),
            pltpu.VMEM((across, lines, band_y), narrow),
        ]
        + [pltpu.SemaphoreType.DMA((c,)) for c in (along, along, across, across)]
        + [pltpu.SemaphoreType.DMA((c,)) for c in (across, across, along, along)],
        compiler_params=pltpu.CompilerParams(collective_id=0, has_side_effects=True),
        name="sum_everywhere",
    )(partial.reshape(pieces))
    return total.reshape(partial.shape).astype(jnp.float32)


def partial_spectrum(scan_data, pixel_coords, aberrations, scan_count):
    pixels, rows, breadth = scan_data.shape
    height = rows * scan_count
    band_x, band_y = height // 2, breadth // 2
    group = 4
    fc, fs = table_pair(centred(breadth), np.arange(breadth), breadth)
    forward = jnp.asarray(np.concatenate([fc.T, -fs.T], axis=1), jnp.bfloat16)
    cc, cs = table_pair(centred(height), np.arange(height), height)
    stacked = np.stack(
        [
            np.concatenate([cc[:, i : i + rows], cs[:, i : i + rows]], axis=1)
            for i in range(0, height, rows)
        ]
    )
    columns = jnp.asarray(stacked, jnp.bfloat16)
    tall = band_x + 2 * REACH
    wide = -(-(band_y + 2 * REACH) // 128) * 128
    whole = lambda shape: pl.BlockSpec(shape, lambda i: (0,) * len(shape))
    shifts = 2 * EXTENT + 1
    return pl.pallas_call(
        functools.partial(partial_kernel, group, rows),
        grid=(pixels // group,),
        out_shape=jax.ShapeDtypeStruct((2, band_x, band_y), jnp.float32),
        in_specs=[
            pl.BlockSpec(memory_space=pltpu.SMEM),
            pl.BlockSpec(memory_space=pltpu.SMEM),
            pl.BlockSpec((group * rows, breadth), lambda i: (i, 0)),
            whole(forward.shape),
            whole(columns.shape),
        ],
        out_specs=whole((2, band_x, band_y)),
        scratch_shapes=[
            pltpu.VMEM((tall, wide), jnp.float32),
            pltpu.VMEM((tall, wide), jnp.float32),
            pltpu.VMEM((shifts, tall, band_y), jnp.float32),
            pltpu.VMEM((shifts, tall, band_y), jnp.float32),
            pltpu.VMEM((group, band_x, 2 * band_y), jnp.float32),
            pltpu.VMEM((2, band_x, band_y), jnp.float32),
        ],
        compiler_params=pltpu.CompilerParams(vmem_limit_bytes=60 * 1024 * 1024),
        name="partial_spectrum",
    )(pixel_coords, aberrations, scan_data.reshape(pixels * rows, breadth), forward, columns)


def on_device(scan_data, pixel_coords, aberrations):
    highest = lax.Precision.HIGHEST
    pixels, rows, breadth = scan_data.shape
    scan_count = lax.axis_size("scan")
    pix_count = lax.axis_size("pix")
    height = rows * scan_count
    partial = partial_spectrum(scan_data, pixel_coords, aberrations, scan_count)
    total = sum_everywhere(partial)
    share = breadth // pix_count
    ic, isn = table_pair(centred(height), np.arange(height), height)
    inverse_x = jnp.asarray(np.stack([ic, isn]), jnp.float32)
    inverse_x = lax.dynamic_slice_in_dim(inverse_x, lax.axis_index("scan") * rows, rows, 2)
    jc, js = table_pair(centred(breadth), np.arange(breadth), breadth)
    inverse_y = jnp.asarray(np.stack([jc, js]), jnp.float32)
    inverse_y = lax.dynamic_slice_in_dim(inverse_y, lax.axis_index("pix") * share, share, 2)
    dot = functools.partial(jnp.einsum, precision=highest)
    left = dot("tkx,pkq->tpxq", inverse_x, total)
    mid_re = left[0, 0] - left[1, 1]
    mid_im = left[1, 0] + left[0, 1]
    mid = jnp.stack([mid_re, mid_im])
    right = dot("pxq,tqy->tpxy", mid, inverse_y)
    result = jnp.stack([right[0, 0] - right[1, 1], right[1, 0] + right[0, 1]])
    return result * (1.0 / (height * breadth))


def solution(mesh):
    placed = (P("pix", "scan", None), P(None, "pix"), P())
    return jax.shard_map(
        on_device, mesh=mesh, in_specs=placed, out_specs=P(None, "scan", "pix"), check_vma=False
    )
```

```python
import functools
import math

import jax
import jax.numpy as jnp
import numpy as np
from jax import lax
from jax.experimental import pallas as pl
from jax.experimental.pallas import tpu as pltpu
from jax.sharding import PartitionSpec as P

STEP = 8
EXTENT = 6
REACH = STEP * EXTENT
APERTURE = 40 * STEP * STEP


def centred(length):
    return np.arange(length // 2) - length // 4


def table_pair(freqs, places, length):
    angles = (np.outer(freqs, places) % length) * (2.0 * math.pi / length)
    return np.cos(angles), np.sin(angles)


def aberration(px, py, a):
    px = px.astype(jnp.float32)
    py = py.astype(jnp.float32)
    radial = (px * px + py * py) / float(APERTURE)
    return (
        a[0] * radial
        + a[1] * (px * px - py * py) / float(APERTURE)
        + a[2] * 2.0 * px * py / float(APERTURE)
        + a[3] * radial * radial
    )


def partial_kernel(
    group, rows, coords, aber, data, forward, columns, final, base_re, base_im, tab_re, tab_im, spec, out
):
    step = pl.program_id(0)
    band_x, band_y = out.shape[1:]
    shifts = tab_re.shape[0]
    coeffs = [aber[i] for i in range(4)]

    @pl.when(step == 0)
    def _():
        out[...] = jnp.zeros_like(out)
        tall, wide = base_re.shape
        chunk = 16

        @pl.loop(0, tall // chunk)
        def _(i):
            at = pl.ds(pl.multiple_of(i * chunk, chunk), chunk)
            px = lax.broadcasted_iota(jnp.int32, (chunk, wide), 0) + (
                i * chunk - band_x // 2 - REACH
            )
            py = lax.broadcasted_iota(jnp.int32, (chunk, wide), 1) - (band_y // 2 + REACH)
            inside = px * px + py * py <= APERTURE
            phase = aberration(px, py, coeffs)
            real = jnp.cos(phase)
            real = jnp.where(real == 0.0, 1e-12, real)
            base_re[at, :] = jnp.where(inside, real, 0.0)
            base_im[at, :] = jnp.where(inside, jnp.sin(phase), 0.0)
            for s in range(shifts):
                tab_re[s, at, :] = base_re[at, STEP * s : STEP * s + band_y]
                tab_im[s, at, :] = base_im[at, STEP * s : STEP * s + band_y]

    me = lax.axis_index("scan")
    table = columns[me]
    rowspec = jnp.dot(data[...], forward[...], preferred_element_type=jnp.float32)

    def transform(g):
        mine = rowspec[g * rows : (g + 1) * rows].astype(jnp.bfloat16)
        turned = jnp.concatenate([mine[:, band_y:], -mine[:, :band_y]], axis=1)
        if rows % 16 == 0:
            both = jnp.concatenate([mine, turned], axis=0)
            spec[g] = jnp.dot(table, both, preferred_element_type=jnp.float32)
        else:
            spec[g] = jnp.dot(
                table[:, :rows], mine, preferred_element_type=jnp.float32
            ) + jnp.dot(table[:, rows:], turned, preferred_element_type=jnp.float32)

    def weigh(g):
        pixel = step * group + g
        u = coords[0, pixel]
        v = coords[1, pixel]
        kx = jnp.full((8, 128), STEP * u, jnp.int32)
        ky = jnp.full((8, 128), STEP * v, jnp.int32)
        own = aberration(kx, ky, coeffs)
        cos_own = jnp.concatenate([jnp.cos(own)] * (band_y // 128), axis=1)
        sin_own = jnp.concatenate([jnp.sin(own)] * (band_y // 128), axis=1)
        for r in range(0, band_x, 8):
            left = pl.ds(pl.multiple_of(r + REACH - STEP * u, 8), 8)
            right = pl.ds(pl.multiple_of(r + REACH + STEP * u, 8), 8)
            ar = tab_re[EXTENT - v, left, :]
            ai = tab_im[EXTENT - v, left, :]
            br = tab_re[EXTENT + v, right, :]
            bi = tab_im[EXTENT + v, right, :]
            both = ar * br != 0.0
            wr = cos_own * (ar - br) + sin_own * (ai - bi)
            wi = cos_own * (ai + bi) - sin_own * (ar + br)
            wr = jnp.where(both, 0.0, wr)
            wi = jnp.where(both, 0.0, wi)
            sr = spec[g, r : r + 8, :band_y]
            si = spec[g, r : r + 8, band_y:]
            out[0, r : r + 8, :] += sr * wr - si * wi
            out[1, r : r + 8, :] += sr * wi + si * wr

    transform(0)
    for g in range(group):
        if g + 1 < group:
            transform(g + 1)
        weigh(g)

    @pl.when(step == pl.num_programs(0) - 1)
    def _():
        final[...] = out[...].astype(final.dtype)


def sum_kernel(along, across, part, total, arrived, held, crossed, own, block, *sems):
    pix_me = lax.axis_index("pix")
    scan_me = lax.axis_index("scan")

    def peer(axis, k):
        if axis == "pix":
            return lax.rem(pix_me + k, across)
        return lax.rem(scan_me + k, along)

    def copy(axis, k, source, target, stage):
        return pltpu.make_async_remote_copy(
            src_ref=source,
            dst_ref=target,
            send_sem=sems[2 * stage].at[k],
            recv_sem=sems[2 * stage + 1].at[k],
            device_id={axis: peer(axis, k)},
            device_id_type=pl.DeviceIdType.MESH,
        )

    barrier = pltpu.get_barrier_semaphore()
    for axis, count in (("pix", across), ("scan", along)):
        for k in range(1, count):
            pl.semaphore_signal(
                barrier,
                inc=1,
                device_id={axis: peer(axis, k)},
                device_id_type=pl.DeviceIdType.MESH,
            )
    pl.semaphore_wait(barrier, across + along - 2)

    pending = [
        copy("pix", k, part.at[peer("pix", k)], arrived.at[k], 0) for k in range(1, across)
    ]
    for c in pending:
        c.start()
    for c in pending:
        c.wait_recv()
    lines = own.shape[0]
    for j in range(along):
        rows = pl.ds(j * lines, lines)
        summed = part[pix_me, rows, :].astype(jnp.float32)
        for k in range(1, across):
            summed += arrived[k, rows, :].astype(jnp.float32)
        held[j] = summed.astype(held.dtype)

    second = [
        copy("scan", k, held.at[peer("scan", k)], crossed.at[k], 1) for k in range(1, along)
    ]
    for c in second:
        c.start()
    for c in second:
        c.wait_recv()
    summed = held[scan_me].astype(jnp.float32)
    for k in range(1, along):
        summed += crossed[k].astype(jnp.float32)
    own[...] = summed.astype(own.dtype)
    block[scan_me] = own[...]

    third = [copy("scan", k, own, block.at[scan_me], 2) for k in range(1, along)]
    for c in third:
        c.start()
    for c in third:
        c.wait_recv()

    fourth = [copy("pix", k, block, total.at[pix_me], 3) for k in range(1, across)]
    for c in fourth:
        c.start()
    total[pix_me] = block[...]
    for c in fourth:
        c.wait_recv()
    for c in pending + second + third + fourth:
        c.wait_send()


def sum_everywhere(partial):
    across = lax.axis_size("pix")
    along = lax.axis_size("scan")
    parts, band_x, band_y = partial.shape
    lines = parts * band_x // (across * along)
    if parts * band_x % (16 * across * along):
        return lax.psum(partial.astype(jnp.float32), ("scan", "pix"))
    narrow = jnp.bfloat16
    pieces = (across, along * lines, band_y)
    vmem = pl.BlockSpec(memory_space=pltpu.VMEM)
    total = pl.pallas_call(
        functools.partial(sum_kernel, along, across),
        out_shape=jax.ShapeDtypeStruct((across, along, lines, band_y), narrow),
        in_specs=[vmem],
        out_specs=vmem,
        scratch_shapes=[
            pltpu.VMEM(pieces, partial.dtype),
            pltpu.VMEM((along, lines, band_y), jnp.float32),
            pltpu.VMEM((along, lines, band_y), jnp.float32),
            pltpu.VMEM((lines, band_y), narrow),
            pltpu.VMEM((along, lines, band_y), narrow),
        ]
        + [pltpu.SemaphoreType.DMA((c,)) for c in (across, across, along, along)]
        + [pltpu.SemaphoreType.DMA((c,)) for c in (along, along, across, across)],
        compiler_params=pltpu.CompilerParams(collective_id=0, has_side_effects=True),
        name="sum_everywhere",
    )(partial.reshape(pieces))
    return total.reshape(partial.shape).astype(jnp.float32)


def partial_spectrum(scan_data, pixel_coords, aberrations, scan_count):
    pixels, rows, breadth = scan_data.shape
    height = rows * scan_count
    band_x, band_y = height // 2, breadth // 2
    group = 4
    fc, fs = table_pair(centred(breadth), np.arange(breadth), breadth)
    forward = jnp.asarray(np.concatenate([fc.T, -fs.T], axis=1), jnp.bfloat16)
    cc, cs = table_pair(centred(height), np.arange(height), height)
    stacked = np.stack(
        [
            np.concatenate([cc[:, i : i + rows], cs[:, i : i + rows]], axis=1)
            for i in range(0, height, rows)
        ]
    )
    columns = jnp.asarray(stacked, jnp.bfloat16)
    tall = band_x + 2 * REACH
    wide = -(-(band_y + 2 * REACH) // 128) * 128
    whole = lambda shape: pl.BlockSpec(shape, lambda i: (0,) * len(shape))
    shifts = 2 * EXTENT + 1
    return pl.pallas_call(
        functools.partial(partial_kernel, group, rows),
        grid=(pixels // group,),
        out_shape=jax.ShapeDtypeStruct((2, band_x, band_y), jnp.bfloat16),
        in_specs=[
            pl.BlockSpec(memory_space=pltpu.SMEM),
            pl.BlockSpec(memory_space=pltpu.SMEM),
            pl.BlockSpec((group * rows, breadth), lambda i: (i, 0)),
            whole(forward.shape),
            whole(columns.shape),
        ],
        out_specs=whole((2, band_x, band_y)),
        scratch_shapes=[
            pltpu.VMEM((tall, wide), jnp.float32),
            pltpu.VMEM((tall, wide), jnp.float32),
            pltpu.VMEM((shifts, tall, band_y), jnp.float32),
            pltpu.VMEM((shifts, tall, band_y), jnp.float32),
            pltpu.VMEM((group, band_x, 2 * band_y), jnp.float32),
            pltpu.VMEM((2, band_x, band_y), jnp.float32),
        ],
        compiler_params=pltpu.CompilerParams(vmem_limit_bytes=60 * 1024 * 1024),
        name="partial_spectrum",
    )(pixel_coords, aberrations, scan_data.reshape(pixels * rows, breadth), forward, columns)


def on_device(scan_data, pixel_coords, aberrations):
    highest = lax.Precision.HIGHEST
    pixels, rows, breadth = scan_data.shape
    scan_count = lax.axis_size("scan")
    pix_count = lax.axis_size("pix")
    height = rows * scan_count
    partial = partial_spectrum(scan_data, pixel_coords, aberrations, scan_count)
    total = sum_everywhere(partial)
    share = breadth // pix_count
    ic, isn = table_pair(centred(height), np.arange(height), height)
    inverse_x = jnp.asarray(np.stack([ic, isn]), jnp.float32)
    inverse_x = lax.dynamic_slice_in_dim(inverse_x, lax.axis_index("scan") * rows, rows, 2)
    jc, js = table_pair(centred(breadth), np.arange(breadth), breadth)
    inverse_y = jnp.asarray(np.stack([jc, js]), jnp.float32)
    inverse_y = lax.dynamic_slice_in_dim(inverse_y, lax.axis_index("pix") * share, share, 2)
    dot = functools.partial(jnp.einsum, precision=highest)
    left = dot("tkx,pkq->tpxq", inverse_x, total)
    mid_re = left[0, 0] - left[1, 1]
    mid_im = left[1, 0] + left[0, 1]
    mid = jnp.stack([mid_re, mid_im])
    right = dot("pxq,tqy->tpxy", mid, inverse_y)
    result = jnp.stack([right[0, 0] - right[1, 1], right[1, 0] + right[0, 1]])
    return result * (1.0 / (height * breadth))


def solution(mesh):
    placed = (P("pix", "scan", None), P(None, "pix"), P())
    return jax.shard_map(
        on_device, mesh=mesh, in_specs=placed, out_specs=P(None, "scan", "pix"), check_vma=False
    )
```

```python
import functools
import math

import jax
import jax.numpy as jnp
import numpy as np
from jax import lax
from jax.experimental import pallas as pl
from jax.experimental.pallas import tpu as pltpu
from jax.sharding import PartitionSpec as P

STEP = 8
EXTENT = 6
REACH = STEP * EXTENT
APERTURE = 40 * STEP * STEP
LIMIT = math.isqrt(APERTURE)


def centred(length):
    return np.arange(length // 2) - length // 4


def table_pair(freqs, places, length):
    angles = (np.outer(freqs, places) % length) * (2.0 * math.pi / length)
    return np.cos(angles), np.sin(angles)


def aberration(px, py, a):
    px = px.astype(jnp.float32)
    py = py.astype(jnp.float32)
    radial = (px * px + py * py) / float(APERTURE)
    return (
        a[0] * radial
        + a[1] * (px * px - py * py) / float(APERTURE)
        + a[2] * 2.0 * px * py / float(APERTURE)
        + a[3] * radial * radial
    )


def partial_kernel(
    group, rows, coords, aber, data, forward, columns, final, base_re, base_im, tab_re, tab_im, spec, out
):
    step = pl.program_id(0)
    band_x, band_y = out.shape[1:]
    shifts = tab_re.shape[0]
    coeffs = [aber[i] for i in range(4)]

    @pl.when(step == 0)
    def _():
        out[...] = jnp.zeros_like(out)
        tall, wide = base_re.shape
        chunk = 16

        @pl.loop(0, tall // chunk)
        def _(i):
            at = pl.ds(pl.multiple_of(i * chunk, chunk), chunk)
            first = i * chunk - band_x // 2 - REACH
            near = jnp.logical_and(first <= LIMIT, first + chunk > -LIMIT)

            @pl.when(jnp.logical_not(near))
            def _():
                for s in range(shifts):
                    tab_re[s, at, :] = jnp.zeros((chunk, band_y), jnp.float32)
                    tab_im[s, at, :] = jnp.zeros((chunk, band_y), jnp.float32)

            @pl.when(near)
            def _():
                px = lax.broadcasted_iota(jnp.int32, (chunk, wide), 0) + (
                    i * chunk - band_x // 2 - REACH
                )
                py = lax.broadcasted_iota(jnp.int32, (chunk, wide), 1) - (band_y // 2 + REACH)
                inside = px * px + py * py <= APERTURE
                phase = aberration(px, py, coeffs)
                real = jnp.cos(phase)
                real = jnp.where(real == 0.0, 1e-12, real)
                base_re[at, :] = jnp.where(inside, real, 0.0)
                base_im[at, :] = jnp.where(inside, jnp.sin(phase), 0.0)
                for s in range(shifts):
                    tab_re[s, at, :] = base_re[at, STEP * s : STEP * s + band_y]
                    tab_im[s, at, :] = base_im[at, STEP * s : STEP * s + band_y]

    me = lax.axis_index("scan")
    table = columns[me]
    rowspec = jnp.dot(data[...], forward[...], preferred_element_type=jnp.float32)

    def transform(g):
        mine = rowspec[g * rows : (g + 1) * rows].astype(jnp.bfloat16)
        turned = jnp.concatenate([mine[:, band_y:], -mine[:, :band_y]], axis=1)
        if rows % 16 == 0:
            both = jnp.concatenate([mine, turned], axis=0)
            spec[g] = jnp.dot(table, both, preferred_element_type=jnp.float32)
        else:
            spec[g] = jnp.dot(
                table[:, :rows], mine, preferred_element_type=jnp.float32
            ) + jnp.dot(table[:, rows:], turned, preferred_element_type=jnp.float32)

    def weigh(g):
        pixel = step * group + g
        u = coords[0, pixel]
        v = coords[1, pixel]
        kx = jnp.full((8, 128), STEP * u, jnp.int32)
        ky = jnp.full((8, 128), STEP * v, jnp.int32)
        own = aberration(kx, ky, coeffs)
        cos_own = jnp.concatenate([jnp.cos(own)] * (band_y // 128), axis=1)
        sin_own = jnp.concatenate([jnp.sin(own)] * (band_y // 128), axis=1)
        for r in range(0, band_x, 8):
            left = pl.ds(pl.multiple_of(r + REACH - STEP * u, 8), 8)
            right = pl.ds(pl.multiple_of(r + REACH + STEP * u, 8), 8)
            ar = tab_re[EXTENT - v, left, :]
            ai = tab_im[EXTENT - v, left, :]
            br = tab_re[EXTENT + v, right, :]
            bi = tab_im[EXTENT + v, right, :]
            both = ar * br != 0.0
            wr = cos_own * (ar - br) + sin_own * (ai - bi)
            wi = cos_own * (ai + bi) - sin_own * (ar + br)
            wr = jnp.where(both, 0.0, wr)
            wi = jnp.where(both, 0.0, wi)
            sr = spec[g, r : r + 8, :band_y]
            si = spec[g, r : r + 8, band_y:]
            out[0, r : r + 8, :] += sr * wr - si * wi
            out[1, r : r + 8, :] += sr * wi + si * wr

    transform(0)
    for g in range(group):
        if g + 1 < group:
            transform(g + 1)
        weigh(g)

    @pl.when(step == pl.num_programs(0) - 1)
    def _():
        final[...] = out[...].astype(final.dtype)


def sum_kernel(along, across, part, total, arrived, held, crossed, own, block, *sems):
    pix_me = lax.axis_index("pix")
    scan_me = lax.axis_index("scan")

    def peer(axis, k):
        if axis == "pix":
            return lax.rem(pix_me + k, across)
        return lax.rem(scan_me + k, along)

    def copy(axis, k, source, target, stage):
        return pltpu.make_async_remote_copy(
            src_ref=source,
            dst_ref=target,
            send_sem=sems[2 * stage].at[k],
            recv_sem=sems[2 * stage + 1].at[k],
            device_id={axis: peer(axis, k)},
            device_id_type=pl.DeviceIdType.MESH,
        )

    barrier = pltpu.get_barrier_semaphore()
    for axis, count in (("pix", across), ("scan", along)):
        for k in range(1, count):
            pl.semaphore_signal(
                barrier,
                inc=1,
                device_id={axis: peer(axis, k)},
                device_id_type=pl.DeviceIdType.MESH,
            )
    pl.semaphore_wait(barrier, across + along - 2)

    pending = [
        copy("pix", k, part.at[peer("pix", k)], arrived.at[k], 0) for k in range(1, across)
    ]
    for c in pending:
        c.start()
    for c in pending:
        c.wait_recv()
    lines = own.shape[0]
    for j in range(along):
        rows = pl.ds(j * lines, lines)
        summed = part[pix_me, rows, :].astype(jnp.float32)
        for k in range(1, across):
            summed += arrived[k, rows, :].astype(jnp.float32)
        held[j] = summed.astype(held.dtype)

    second = [
        copy("scan", k, held.at[peer("scan", k)], crossed.at[k], 1) for k in range(1, along)
    ]
    for c in second:
        c.start()
    for c in second:
        c.wait_recv()
    summed = held[scan_me].astype(jnp.float32)
    for k in range(1, along):
        summed += crossed[k].astype(jnp.float32)
    own[...] = summed.astype(own.dtype)
    block[scan_me] = own[...]

    third = [copy("scan", k, own, block.at[scan_me], 2) for k in range(1, along)]
    for c in third:
        c.start()
    for c in third:
        c.wait_recv()

    fourth = [copy("pix", k, block, total.at[pix_me], 3) for k in range(1, across)]
    for c in fourth:
        c.start()
    total[pix_me] = block[...]
    for c in fourth:
        c.wait_recv()
    for c in pending + second + third + fourth:
        c.wait_send()


def sum_everywhere(partial):
    across = lax.axis_size("pix")
    along = lax.axis_size("scan")
    parts, band_x, band_y = partial.shape
    lines = parts * band_x // (across * along)
    if parts * band_x % (16 * across * along):
        return lax.psum(partial.astype(jnp.float32), ("scan", "pix"))
    narrow = jnp.bfloat16
    pieces = (across, along * lines, band_y)
    vmem = pl.BlockSpec(memory_space=pltpu.VMEM)
    total = pl.pallas_call(
        functools.partial(sum_kernel, along, across),
        out_shape=jax.ShapeDtypeStruct((across, along, lines, band_y), narrow),
        in_specs=[vmem],
        out_specs=vmem,
        scratch_shapes=[
            pltpu.VMEM(pieces, partial.dtype),
            pltpu.VMEM((along, lines, band_y), jnp.float32),
            pltpu.VMEM((along, lines, band_y), jnp.float32),
            pltpu.VMEM((lines, band_y), narrow),
            pltpu.VMEM((along, lines, band_y), narrow),
        ]
        + [pltpu.SemaphoreType.DMA((c,)) for c in (across, across, along, along)]
        + [pltpu.SemaphoreType.DMA((c,)) for c in (along, along, across, across)],
        compiler_params=pltpu.CompilerParams(collective_id=0, has_side_effects=True),
        name="sum_everywhere",
    )(partial.reshape(pieces))
    return total.reshape(partial.shape).astype(jnp.float32)


def partial_spectrum(scan_data, pixel_coords, aberrations, scan_count):
    pixels, rows, breadth = scan_data.shape
    height = rows * scan_count
    band_x, band_y = height // 2, breadth // 2
    group = 4
    fc, fs = table_pair(centred(breadth), np.arange(breadth), breadth)
    forward = jnp.asarray(np.concatenate([fc.T, -fs.T], axis=1), jnp.bfloat16)
    cc, cs = table_pair(centred(height), np.arange(height), height)
    stacked = np.stack(
        [
            np.concatenate([cc[:, i : i + rows], cs[:, i : i + rows]], axis=1)
            for i in range(0, height, rows)
        ]
    )
    columns = jnp.asarray(stacked, jnp.bfloat16)
    tall = band_x + 2 * REACH
    wide = -(-(band_y + 2 * REACH) // 128) * 128
    whole = lambda shape: pl.BlockSpec(shape, lambda i: (0,) * len(shape))
    shifts = 2 * EXTENT + 1
    return pl.pallas_call(
        functools.partial(partial_kernel, group, rows),
        grid=(pixels // group,),
        out_shape=jax.ShapeDtypeStruct((2, band_x, band_y), jnp.bfloat16),
        in_specs=[
            pl.BlockSpec(memory_space=pltpu.SMEM),
            pl.BlockSpec(memory_space=pltpu.SMEM),
            pl.BlockSpec((group * rows, breadth), lambda i: (i, 0)),
            whole(forward.shape),
            whole(columns.shape),
        ],
        out_specs=whole((2, band_x, band_y)),
        scratch_shapes=[
            pltpu.VMEM((tall, wide), jnp.float32),
            pltpu.VMEM((tall, wide), jnp.float32),
            pltpu.VMEM((shifts, tall, band_y), jnp.float32),
            pltpu.VMEM((shifts, tall, band_y), jnp.float32),
            pltpu.VMEM((group, band_x, 2 * band_y), jnp.float32),
            pltpu.VMEM((2, band_x, band_y), jnp.float32),
        ],
        compiler_params=pltpu.CompilerParams(vmem_limit_bytes=60 * 1024 * 1024),
        name="partial_spectrum",
    )(pixel_coords, aberrations, scan_data.reshape(pixels * rows, breadth), forward, columns)


def on_device(scan_data, pixel_coords, aberrations):
    highest = lax.Precision.HIGHEST
    pixels, rows, breadth = scan_data.shape
    scan_count = lax.axis_size("scan")
    pix_count = lax.axis_size("pix")
    height = rows * scan_count
    partial = partial_spectrum(scan_data, pixel_coords, aberrations, scan_count)
    total = sum_everywhere(partial)
    share = breadth // pix_count
    scale = 1.0 / (height * breadth)
    ic, isn = table_pair(centred(height), np.arange(height), height)
    inverse_x = jnp.asarray(np.stack([np.stack([ic, -isn]), np.stack([isn, ic])]), jnp.float32)
    inverse_x = lax.dynamic_slice_in_dim(inverse_x, lax.axis_index("scan") * rows, rows, 3)
    jc, js = table_pair(centred(breadth), np.arange(breadth), breadth)
    inverse_y = np.stack([np.stack([jc, -js]), np.stack([js, jc])])
    inverse_y = jnp.asarray(inverse_y * scale, jnp.float32)
    inverse_y = lax.dynamic_slice_in_dim(inverse_y, lax.axis_index("pix") * share, share, 3)
    dot = functools.partial(jnp.einsum, precision=highest)
    middle = dot("tpkx,pkq->txq", inverse_x, total)
    return dot("pxq,tpqy->txy", middle, inverse_y)


def solution(mesh):
    placed = (P("pix", "scan", None), P(None, "pix"), P())
    return jax.shard_map(
        on_device, mesh=mesh, in_specs=placed, out_specs=P(None, "scan", "pix"), check_vma=False
    )
```

```python
import functools
import math

import jax
import jax.numpy as jnp
import numpy as np
from jax import lax
from jax.experimental import pallas as pl
from jax.experimental.pallas import tpu as pltpu
from jax.sharding import PartitionSpec as P

STEP = 8
EXTENT = 6
REACH = STEP * EXTENT
APERTURE = 40 * STEP * STEP
LIMIT = math.isqrt(APERTURE)


def centred(length):
    return np.arange(length // 2) - length // 4


def table_pair(freqs, places, length):
    angles = (np.outer(freqs, places) % length) * (2.0 * math.pi / length)
    return np.cos(angles), np.sin(angles)


def aberration(px, py, a):
    px = px.astype(jnp.float32)
    py = py.astype(jnp.float32)
    radial = (px * px + py * py) / float(APERTURE)
    return (
        a[0] * radial
        + a[1] * (px * px - py * py) / float(APERTURE)
        + a[2] * 2.0 * px * py / float(APERTURE)
        + a[3] * radial * radial
    )


def partial_kernel(
    group, rows, coords, aber, data, forward, columns, final, base_re, base_im, tab_re, tab_im, spec, out
):
    step = pl.program_id(0)
    band_x, band_y = out.shape[1:]
    shifts = tab_re.shape[0]
    coeffs = [aber[i] for i in range(4)]

    @pl.when(step == 0)
    def _():
        out[...] = jnp.zeros_like(out)
        tall, wide = base_re.shape
        chunk = 16
        used = min(wide, -(-(band_y // 2 + REACH + LIMIT + 1) // 128) * 128)

        @pl.loop(0, tall // chunk)
        def _(i):
            at = pl.ds(pl.multiple_of(i * chunk, chunk), chunk)
            first = i * chunk - band_x // 2 - REACH
            near = jnp.logical_and(first <= LIMIT, first + chunk > -LIMIT)

            @pl.when(jnp.logical_not(near))
            def _():
                for s in range(shifts):
                    tab_re[s, at, :] = jnp.zeros((chunk, band_y), jnp.float32)
                    tab_im[s, at, :] = jnp.zeros((chunk, band_y), jnp.float32)

            @pl.when(near)
            def _():
                px = lax.broadcasted_iota(jnp.int32, (chunk, used), 0) + (
                    i * chunk - band_x // 2 - REACH
                )
                py = lax.broadcasted_iota(jnp.int32, (chunk, used), 1) - (band_y // 2 + REACH)
                inside = px * px + py * py <= APERTURE
                phase = aberration(px, py, coeffs)
                real = jnp.cos(phase)
                real = jnp.where(real == 0.0, 1e-12, real)
                base_re[at, :used] = jnp.where(inside, real, 0.0)
                base_im[at, :used] = jnp.where(inside, jnp.sin(phase), 0.0)
                if used < wide:
                    base_re[at, used:] = jnp.zeros((chunk, wide - used), jnp.float32)
                    base_im[at, used:] = jnp.zeros((chunk, wide - used), jnp.float32)
                for s in range(shifts):
                    tab_re[s, at, :] = base_re[at, STEP * s : STEP * s + band_y]
                    tab_im[s, at, :] = base_im[at, STEP * s : STEP * s + band_y]

    me = lax.axis_index("scan")
    table = columns[me]
    rowspec = jnp.dot(data[...], forward[...], preferred_element_type=jnp.float32)

    def transform(g):
        mine = rowspec[g * rows : (g + 1) * rows].astype(jnp.bfloat16)
        turned = jnp.concatenate([mine[:, band_y:], -mine[:, :band_y]], axis=1)
        if rows % 16 == 0:
            both = jnp.concatenate([mine, turned], axis=0)
            spec[g] = jnp.dot(table, both, preferred_element_type=jnp.float32)
        else:
            spec[g] = jnp.dot(
                table[:, :rows], mine, preferred_element_type=jnp.float32
            ) + jnp.dot(table[:, rows:], turned, preferred_element_type=jnp.float32)

    def weigh(g):
        pixel = step * group + g
        u = coords[0, pixel]
        v = coords[1, pixel]
        kx = jnp.full((8, 128), STEP * u, jnp.int32)
        ky = jnp.full((8, 128), STEP * v, jnp.int32)
        own = aberration(kx, ky, coeffs)
        cos_own = jnp.concatenate([jnp.cos(own)] * (band_y // 128), axis=1)
        sin_own = jnp.concatenate([jnp.sin(own)] * (band_y // 128), axis=1)
        for r in range(0, band_x, 8):
            left = pl.ds(pl.multiple_of(r + REACH - STEP * u, 8), 8)
            right = pl.ds(pl.multiple_of(r + REACH + STEP * u, 8), 8)
            ar = tab_re[EXTENT - v, left, :]
            ai = tab_im[EXTENT - v, left, :]
            br = tab_re[EXTENT + v, right, :]
            bi = tab_im[EXTENT + v, right, :]
            both = ar * br != 0.0
            wr = cos_own * (ar - br) + sin_own * (ai - bi)
            wi = cos_own * (ai + bi) - sin_own * (ar + br)
            wr = jnp.where(both, 0.0, wr)
            wi = jnp.where(both, 0.0, wi)
            sr = spec[g, r : r + 8, :band_y]
            si = spec[g, r : r + 8, band_y:]
            out[0, r : r + 8, :] += sr * wr - si * wi
            out[1, r : r + 8, :] += sr * wi + si * wr

    transform(0)
    for g in range(group):
        if g + 1 < group:
            transform(g + 1)
        weigh(g)

    @pl.when(step == pl.num_programs(0) - 1)
    def _():
        final[...] = out[...].astype(final.dtype)


def sum_kernel(along, across, part, total, arrived, held, crossed, own, block, *sems):
    pix_me = lax.axis_index("pix")
    scan_me = lax.axis_index("scan")

    def peer(axis, k):
        if axis == "pix":
            return lax.rem(pix_me + k, across)
        return lax.rem(scan_me + k, along)

    def copy(axis, k, source, target, stage):
        return pltpu.make_async_remote_copy(
            src_ref=source,
            dst_ref=target,
            send_sem=sems[2 * stage].at[k],
            recv_sem=sems[2 * stage + 1].at[k],
            device_id={axis: peer(axis, k)},
            device_id_type=pl.DeviceIdType.MESH,
        )

    barrier = pltpu.get_barrier_semaphore()
    for axis, count in (("pix", across), ("scan", along)):
        for k in range(1, count):
            pl.semaphore_signal(
                barrier,
                inc=1,
                device_id={axis: peer(axis, k)},
                device_id_type=pl.DeviceIdType.MESH,
            )
    pl.semaphore_wait(barrier, across + along - 2)

    pending = [
        copy("pix", k, part.at[peer("pix", k)], arrived.at[k], 0) for k in range(1, across)
    ]
    for c in pending:
        c.start()
    for c in pending:
        c.wait_recv()
    lines = own.shape[0]
    for j in range(along):
        rows = pl.ds(j * lines, lines)
        summed = part[pix_me, rows, :].astype(jnp.float32)
        for k in range(1, across):
            summed += arrived[k, rows, :].astype(jnp.float32)
        held[j] = summed.astype(held.dtype)

    second = [
        copy("scan", k, held.at[peer("scan", k)], crossed.at[k], 1) for k in range(1, along)
    ]
    for c in second:
        c.start()
    for c in second:
        c.wait_recv()
    summed = held[scan_me].astype(jnp.float32)
    for k in range(1, along):
        summed += crossed[k].astype(jnp.float32)
    own[...] = summed.astype(own.dtype)
    block[scan_me] = own[...]

    third = [copy("scan", k, own, block.at[scan_me], 2) for k in range(1, along)]
    for c in third:
        c.start()
    for c in third:
        c.wait_recv()

    fourth = [copy("pix", k, block, total.at[pix_me], 3) for k in range(1, across)]
    for c in fourth:
        c.start()
    total[pix_me] = block[...]
    for c in fourth:
        c.wait_recv()
    for c in pending + second + third + fourth:
        c.wait_send()


def sum_everywhere(partial):
    across = lax.axis_size("pix")
    along = lax.axis_size("scan")
    parts, band_x, band_y = partial.shape
    lines = parts * band_x // (across * along)
    if parts * band_x % (16 * across * along):
        return lax.psum(partial.astype(jnp.float32), ("scan", "pix"))
    narrow = jnp.bfloat16
    pieces = (across, along * lines, band_y)
    vmem = pl.BlockSpec(memory_space=pltpu.VMEM)
    total = pl.pallas_call(
        functools.partial(sum_kernel, along, across),
        out_shape=jax.ShapeDtypeStruct((across, along, lines, band_y), narrow),
        in_specs=[vmem],
        out_specs=vmem,
        scratch_shapes=[
            pltpu.VMEM(pieces, partial.dtype),
            pltpu.VMEM((along, lines, band_y), jnp.float32),
            pltpu.VMEM((along, lines, band_y), jnp.float32),
            pltpu.VMEM((lines, band_y), narrow),
            pltpu.VMEM((along, lines, band_y), narrow),
        ]
        + [pltpu.SemaphoreType.DMA((c,)) for c in (across, across, along, along)]
        + [pltpu.SemaphoreType.DMA((c,)) for c in (along, along, across, across)],
        compiler_params=pltpu.CompilerParams(collective_id=0, has_side_effects=True),
        name="sum_everywhere",
    )(partial.reshape(pieces))
    return total.reshape(partial.shape).astype(jnp.float32)


def partial_spectrum(scan_data, pixel_coords, aberrations, scan_count):
    pixels, rows, breadth = scan_data.shape
    height = rows * scan_count
    band_x, band_y = height // 2, breadth // 2
    group = 4
    fc, fs = table_pair(centred(breadth), np.arange(breadth), breadth)
    forward = jnp.asarray(np.concatenate([fc.T, -fs.T], axis=1), jnp.bfloat16)
    cc, cs = table_pair(centred(height), np.arange(height), height)
    stacked = np.stack(
        [
            np.concatenate([cc[:, i : i + rows], cs[:, i : i + rows]], axis=1)
            for i in range(0, height, rows)
        ]
    )
    columns = jnp.asarray(stacked, jnp.bfloat16)
    tall = band_x + 2 * REACH
    wide = -(-(band_y + 2 * REACH) // 128) * 128
    whole = lambda shape: pl.BlockSpec(shape, lambda i: (0,) * len(shape))
    shifts = 2 * EXTENT + 1
    return pl.pallas_call(
        functools.partial(partial_kernel, group, rows),
        grid=(pixels // group,),
        out_shape=jax.ShapeDtypeStruct((2, band_x, band_y), jnp.bfloat16),
        in_specs=[
            pl.BlockSpec(memory_space=pltpu.SMEM),
            pl.BlockSpec(memory_space=pltpu.SMEM),
            pl.BlockSpec((group * rows, breadth), lambda i: (i, 0)),
            whole(forward.shape),
            whole(columns.shape),
        ],
        out_specs=whole((2, band_x, band_y)),
        scratch_shapes=[
            pltpu.VMEM((tall, wide), jnp.float32),
            pltpu.VMEM((tall, wide), jnp.float32),
            pltpu.VMEM((shifts, tall, band_y), jnp.float32),
            pltpu.VMEM((shifts, tall, band_y), jnp.float32),
            pltpu.VMEM((group, band_x, 2 * band_y), jnp.float32),
            pltpu.VMEM((2, band_x, band_y), jnp.float32),
        ],
        compiler_params=pltpu.CompilerParams(vmem_limit_bytes=60 * 1024 * 1024),
        name="partial_spectrum",
    )(pixel_coords, aberrations, scan_data.reshape(pixels * rows, breadth), forward, columns)


def on_device(scan_data, pixel_coords, aberrations):
    highest = lax.Precision.HIGHEST
    pixels, rows, breadth = scan_data.shape
    scan_count = lax.axis_size("scan")
    pix_count = lax.axis_size("pix")
    height = rows * scan_count
    partial = partial_spectrum(scan_data, pixel_coords, aberrations, scan_count)
    total = sum_everywhere(partial)
    share = breadth // pix_count
    ic, isn = table_pair(centred(height), np.arange(height), height)
    inverse_x = jnp.asarray(np.stack([ic, isn]), jnp.float32)
    inverse_x = lax.dynamic_slice_in_dim(inverse_x, lax.axis_index("scan") * rows, rows, 2)
    jc, js = table_pair(centred(breadth), np.arange(breadth), breadth)
    inverse_y = jnp.asarray(np.stack([jc, js]) * (1.0 / (height * breadth)), jnp.float32)
    inverse_y = lax.dynamic_slice_in_dim(inverse_y, lax.axis_index("pix") * share, share, 2)
    dot = functools.partial(jnp.einsum, precision=highest)
    left = dot("tkx,pkq->tpxq", inverse_x, total)
    mid_re = left[0, 0] - left[1, 1]
    mid_im = left[1, 0] + left[0, 1]
    mid = jnp.stack([mid_re, mid_im])
    right = dot("pxq,tqy->tpxy", mid, inverse_y)
    result = jnp.stack([right[0, 0] - right[1, 1], right[1, 0] + right[0, 1]])
    return result


def solution(mesh):
    placed = (P("pix", "scan", None), P(None, "pix"), P())
    return jax.shard_map(
        on_device, mesh=mesh, in_specs=placed, out_specs=P(None, "scan", "pix"), check_vma=False
    )
```
